256 devices in a mesh: section: 4 (over y), expert: 64 (over z, x, core).
Axes of the slice: x: 4, y: 4, z: 8, core: 2. Of those that a mesh axis runs over, the one named last changes fastest.
Arguments:
- fresh: bfloat16 [8192, 2048], P('expert'), may hold values from -6 to 6
- previous: bfloat16 [4, 8192, 2048], P('section', 'expert'), may hold values from -6 to 6
- norm_gain: float32 [4, 2048], P('section'), may hold values from 0.1 to 1.9
- routes: int32 [4, 8192, 8], P('section', 'expert'), may hold values from 0 to 63, all different within a row; in each aligned block of 128 rows (0 to 127, 128 to 255, ..., all dimensions but the last counted through in order) at most 17 rows name the same one
- gate_weights: float32 [4, 8192, 8], P('section', 'expert'), may hold values from 0.03 to 0.3
- w_gate_up: bfloat16 [4, 64, 2048, 1536], P('section', 'expert'), may hold values from -0.125 to 0.125
- w_down: bfloat16 [4, 64, 768, 2048], P('section', 'expert'), may hold values from -0.21875 to 0.21875
Outputs:
- section_output: bfloat16 [4, 8192, 2048], P('section', 'expert')
The draws below stay inside these ranges and needn't reach their ends.
Inputs may be any that keep to these rules, and one draw needn't show every extreme that they name: `routes`: within one section, among the 128 tokens of one device (aligned blocks of tokens) no expert is chosen by more than 17 tokens, and some expert is chosen by exactly 17 of them; the 8 experts of a token differ.
All inputs are finite; a program needn't handle non-finite values.
Results may differ from the reference program's by a relative error of at most 0.0033.
Values may be sent and summed in bfloat16 or wider, within the bound.
A program may use at most 64 MiB of HBM per device.

```python
import math
import jax
import jax.numpy as jnp
import numpy as np
from jax import lax

D = 2048
F = 768
TOPK = 8
TOK_DEV = 128
SECTIONS = 4
EXPERTS = 64
TOKENS = 8192
CAP = 17
ROWS_MAX = 1088


def levels(stream_key, extent, pieces, smallest, top_value):
    level, own = 1.0, jax.random.fold_in(stream_key, 6)
    for dim, parts in pieces:
        steps = jnp.exp(jax.random.uniform(jax.random.fold_in(own, dim), (parts,), jnp.float32, smallest / len(pieces), top_value / len(pieces)))
        level = level * jnp.repeat(steps, extent[dim] // parts).reshape([-1 if axis == dim else 1 for axis in range(len(extent))])
    return level


def routed_block(own_key, own, number, rows, amount, top, limit, lean):
    sequence = jax.random.permutation(own_key, amount)
    heavy_load, usual = load_shares(amount, rows * top, limit, lean, True), load_shares(amount, rows * top, limit, lean, False)
    places = jnp.arange(amount)

    def named(lengths, rotation):
        used = int((lengths > 0).sum())
        fixed = max(1, used // 4)
        moved = fixed + (places - fixed + rotation * (used - fixed)) % max(1, amount - fixed)
        return jnp.zeros((amount,), jnp.int32).at[sequence[jnp.where(places < fixed, places, moved)]].set(jnp.asarray(lengths, jnp.int32))

    lengths = jnp.where(number % 4 == 0, named(heavy_load, number // 4), named(usual, number - number // 4 - 1))
    mixed = jax.random.permutation(jax.random.fold_in(own, 3), amount)
    source_of, taker = mixed[0:amount // 2 * 2:2], mixed[1:amount // 2 * 2:2]
    slack = jnp.minimum(lengths[source_of] - 1, limit - lengths[taker]) // 2
    slack = jnp.where((source_of == sequence[0]) | (taker == sequence[0]) | (lengths[taker] == 0), 0, jnp.maximum(slack, 0))
    moved = jax.random.randint(jax.random.fold_in(own, 4), (amount // 2,), 0, 1 << 20) % (slack + 1)
    lengths = lengths.at[source_of].add(-moved).at[taker].add(moved)
    labels = jnp.searchsorted(jnp.cumsum(lengths), jnp.arange(rows * top), side="right").astype(jnp.int32)
    table = labels.reshape(top, rows).T
    table = table[jax.random.permutation(jax.random.fold_in(own, 1), rows)]
    rotation = jax.random.randint(jax.random.fold_in(own, 2), (rows, 1), 0, top)
    return jnp.take_along_axis(table, (jnp.arange(top)[None, :] + rotation) % top, axis=1)


def load_shares(number_of, total, most, slope, full):
    portions = [(1 << 20) // math.isqrt(grade ** slope) + 1 for grade in range(1, number_of + 1)]
    largest = most if full else min(most, max(-(-total // number_of), total * portions[0] // sum(portions)))
    least = 1 if total - largest >= number_of - 1 else 0
    counts, surplus = [largest] + [least] * (number_of - 1), total - largest - least * (number_of - 1)
    while surplus > 0:
        candidates = [i for i in range(1, number_of) if counts[i] < largest] or [i for i in range(1, number_of) if counts[i] < most]
        mass, remaining = sum([portions[i] for i in candidates]), surplus
        for i in candidates:
            more = min(most - counts[i], max(1, remaining * portions[i] // mass), surplus)
            counts[i] = counts[i] + more
            surplus = surplus - more
    return np.array(counts)


def scatter_about(stream_key, dims, scale, limit, shards=(), kind=jnp.bfloat16):
    loudness = levels(stream_key, dims, shards, -0.22, 0.18) if shards else 1.0
    entries = jax.random.normal(stream_key, dims, jnp.float32) * scale * loudness
    return jnp.minimum(jnp.maximum(entries, -limit), limit).astype(kind)


def setup_inputs(seed: int = 0) -> dict:
    key_of = jax.random.split(jax.random.key(seed), 8)
    fresh = scatter_about(key_of[0], (TOKENS, D), 1.0, 6.0, ((0, 64),))
    previous = scatter_about(key_of[1], (SECTIONS, TOKENS, D), 1.0, 6.0, ((0, 4), (1, 64)))
    norm_gain = jnp.clip(1.0 + 0.18 * jax.random.normal(key_of[2], (SECTIONS, D), jnp.float32), 0.1, 1.9)
    routes_keys = jax.random.split(jax.random.fold_in(key_of[3], 1), SECTIONS * TOKENS // TOK_DEV)
    routes_turns = jax.random.permutation(jax.random.fold_in(key_of[3], 3), SECTIONS * TOKENS // TOK_DEV)
    routes = jax.vmap(lambda own, number: routed_block(jax.random.fold_in(key_of[3], 2), own, number, TOK_DEV, EXPERTS, TOPK, CAP, 2))(routes_keys, routes_turns).reshape((SECTIONS, TOKENS, TOPK))
    gate_weights = jnp.clip(jnp.exp(math.log(0.3) - 2.3025852 * jax.random.uniform(key_of[4], (SECTIONS, TOKENS, TOPK), jnp.float32) ** levels(key_of[4], (SECTIONS, TOKENS, TOPK), ((0, 4), (1, 64)), -0.2, 0.2)), 0.03, 0.3)
    w_gate_up = scatter_about(key_of[5], (SECTIONS, EXPERTS, D, 2 * F), D ** -0.5, 0.125, ((0, 4), (1, 64)))
    w_down = scatter_about(key_of[6], (SECTIONS, EXPERTS, F, D), F ** -0.5, 0.21875, ((0, 4), (1, 64)))
    return dict(fresh=fresh, previous=previous, norm_gain=norm_gain, routes=routes, gate_weights=gate_weights, w_gate_up=w_gate_up, w_down=w_down)


epsilon = 1e-06

def one_layer(arrival, gain, route_ids, gates, gate_up, down):
    wide_input = arrival.astype(jnp.float32)
    scale = lax.rsqrt(lax.optimization_barrier(jnp.mean(wide_input * wide_input, axis=-1, keepdims=True)) + epsilon)
    normed = (wide_input * scale * gain[None, :]).astype(jnp.bfloat16)
    flat_ids = route_ids.reshape(-1).astype(jnp.int32)
    total_rows = flat_ids.shape[0]
    padded = jnp.concatenate([normed, jnp.zeros((1, D), jnp.bfloat16)], axis=0)

    def run_expert(expert_num):
        row_index = jnp.nonzero(flat_ids == expert_num, size=ROWS_MAX, fill_value=total_rows)[0].astype(jnp.int32)
        rows = padded[row_index // TOPK]
        projected = jnp.dot(rows, gate_up[expert_num], preferred_element_type=jnp.float32)
        hidden = (jax.nn.silu(projected[:, :F]) * projected[:, F:]).astype(jnp.bfloat16)
        result = jnp.dot(hidden, down[expert_num], preferred_element_type=jnp.float32).astype(jnp.bfloat16)
        return (row_index, result)
    indices, results = lax.map(run_expert, jnp.arange(EXPERTS, dtype=jnp.int32))
    table = jnp.zeros((total_rows + 1, D), jnp.bfloat16).at[indices.reshape(-1)].set(results.reshape(-1, D))
    picked = table[:total_rows].reshape(TOKENS, TOPK, D).astype(jnp.float32)
    mixed = lax.optimization_barrier(jnp.sum(picked * gates[:, :, None], axis=1))
    return (wide_input + mixed).astype(jnp.bfloat16)

def reference(fresh, previous, norm_gain, routes, gate_weights, w_gate_up, w_down):
    layers_out = []
    for section_num in range(SECTIONS):
        arrival = fresh if section_num == 0 else previous[section_num - 1]
        layers_out.append(one_layer(arrival, norm_gain[section_num], routes[section_num], gate_weights[section_num], w_gate_up[section_num], w_down[section_num]))
    return jnp.stack(layers_out, axis=0)
```

```python
import functools

import jax
import jax.numpy as jnp
from jax import lax
from jax.experimental import pallas as pl
from jax.experimental.pallas import tpu as pltpu
from jax.sharding import PartitionSpec as P

EPS = 1e-06
SLOT = 16
MESH = pl.DeviceIdType.MESH
F32, BF16 = jnp.float32, jnp.bfloat16


def kernel(
    Z, J, K,
    prev, fresh, gain, aux, wgu_h, wd_h, out,
    wgu, wd, fr, yr, arr, ag, auxb, x1s, x1r, yb, x2r, rss, rsr, hid, pf, sel8, ranks, gates,
    ysem, yrem, lsem, zss, zrs, axs, axr, x1ss, x1rs, x2ss, x2rs, rsss, rsrs,
):
    T, D = arr.shape
    HT = T // 2
    F = wd.shape[0]
    R = J * SLOT
    TN = min(512, D)
    TF = min(256, F)
    sec, nsec = lax.axis_index("section"), lax.axis_size("section")
    e = lax.axis_index("expert")
    z, j = lax.div(e, J), lax.rem(e, J)
    up = lax.rem(z + 1, Z) * J + j
    dn = lax.rem(z + Z - 1, Z) * J + j
    ynext, yprev = lax.rem(sec + 1, nsec), lax.rem(sec + nsec - 1, nsec)
    toward = (up, dn)
    half = (pl.ds(0, HT), pl.ds(HT, HT))
    order = [q for q in (4, 2, 6, 5, 3, 7, 1) if q < J]

    def remote(src, dst, ssem, rsem, expert):
        return pltpu.make_async_remote_copy(
            src_ref=src, dst_ref=dst, send_sem=ssem, recv_sem=rsem,
            device_id={"expert": expert}, device_id_type=MESH)

    loads = (
        pltpu.make_async_copy(fresh, fr, lsem.at[0]),
        pltpu.make_async_copy(wgu_h.at[0, 0], wgu, lsem.at[1]),
        pltpu.make_async_copy(wd_h.at[0, 0], wd, lsem.at[2]),
    )
    for c in loads:
        c.start()

    barrier = pltpu.get_barrier_semaphore()
    for t in (up, dn):
        pl.semaphore_signal(barrier, inc=1, device_id={"expert": t}, device_id_type=MESH)
    for q in order:
        pl.semaphore_signal(
            barrier, inc=1, device_id={"expert": z * J + lax.rem(j + q, J)}, device_id_type=MESH)
    for t in (ynext, yprev):
        pl.semaphore_signal(barrier, inc=1, device_id={"section": t}, device_id_type=MESH)
    pl.semaphore_wait(barrier, 4 + len(order))

    ycopies = [
        pltpu.make_async_remote_copy(
            src_ref=prev.at[0, half[h]], dst_ref=yr.at[half[h]], send_sem=ysem.at[h],
            recv_sem=yrem.at[h], device_id={"section": ynext}, device_id_type=MESH)
        for h in range(2)
    ]
    for c in ycopies:
        c.start()

    def zcopy(d, k, h, src):
        dst = 2 * k - 1 if d == 0 else jnp.minimum(2 * k, 7)
        return remote(ag.at[src, half[h]], ag.at[dst, half[h]], zss.at[d, k - 1, h],
                      zrs.at[d, k - 1, h], toward[d])

    def acopy(d, k, src):
        dst = 2 * k - 1 if d == 0 else jnp.minimum(2 * k, 7)
        return remote(auxb.at[src], auxb.at[dst], axs.at[d, k - 1], axr.at[d, k - 1], toward[d])

    auxb[0] = aux[...]
    acopy(0, 1, 0).start()
    acopy(1, 1, 0).start()
    loads[0].wait()
    for h in range(2):
        ycopies[h].wait_recv()
        x = jnp.where(sec == 0, fr[half[h], :].astype(F32), yr[half[h], :].astype(F32))
        arr[half[h], :] = x.astype(BF16)
        scale = lax.rsqrt(jnp.mean(x * x, axis=-1, keepdims=True) + EPS)
        ag[0, half[h], :] = (x * scale * gain[...]).astype(BF16)
        zcopy(0, 1, h, 0).start()
        zcopy(1, 1, h, 0).start()

    slot3 = lax.broadcasted_iota(jnp.int32, (J, SLOT, T), 1).astype(F32)
    first = (z * J).astype(F32)

    def own_rows(q):
        return pl.ds(pl.multiple_of(q * SLOT, SLOT), SLOT)

    def xcopy(src, dst, ssem, rsem, v, q):
        pj = lax.rem(j + q, J)
        return remote(src.at[v, own_rows(pj)], dst.at[v, own_rows(j)], ssem.at[v], rsem.at[v],
                      z * J + pj)

    def xwait(buf, sem, v):
        part = buf.at[v, pl.ds(0, R - SLOT)]
        pltpu.make_async_copy(part, part, sem.at[v]).wait()

    def xsend(src, dst, ssem, rsem, v):
        dst[v, own_rows(j), :] = src[v, own_rows(j), :]
        for q in order:
            xcopy(src, dst, ssem, rsem, v, q).start()

    def pick(matrix, source, v):
        def tile(n, _):
            c = pl.ds(pl.multiple_of(n * TN, TN), TN)
            x1s[v, :, c] = jnp.dot(matrix, source(c), preferred_element_type=F32).astype(BF16)
            return 0
        lax.fori_loop(0, D // TN, tile, 0)
        xsend(x1s, x1r, x1ss, x1rs, v)

    def select(u):
        a = auxb[u]
        expert = lax.broadcasted_iota(jnp.int32, (J, T), 0).astype(F32) + first
        mask, gate = jnp.zeros((J, T), F32), jnp.zeros((J, T), F32)
        for k in range(K):
            hit = a[k:k + 1, :] == expert
            mask = mask + jnp.where(hit, 1.0, 0.0)
            gate = gate + jnp.where(hit, a[8 + k:9 + k, :], 0.0)
        before = (lax.broadcasted_iota(jnp.int32, (T, T), 0)
                  < lax.broadcasted_iota(jnp.int32, (T, T), 1))
        tri = jnp.where(before, 1.0, 0.0).astype(BF16)
        rank = jnp.dot(mask.astype(BF16), tri, preferred_element_type=F32)
        rank = jnp.where(mask > 0.5, rank, -1.0)
        ranks[u] = rank
        gates[u] = gate
        r3 = jnp.broadcast_to(rank[:, None, :], (J, SLOT, T))
        uf = jnp.asarray(u, jnp.int32).astype(F32)
        sel = jnp.where(r3 == slot3, 1.0, 0.0).reshape(R, T).astype(BF16)
        extra = jnp.where(r3 == float(SLOT), 1.0, 0.0) * jnp.where(slot3 == uf, 1.0, 0.0)
        sel8[:, pl.ds(pl.multiple_of(u * T, T), T)] = extra.reshape(R, T).astype(BF16)
        pick(sel, lambda c: ag[u, :, c], u + 1)

    def ffn(v):
        def rise(n, _):
            lo = pl.ds(pl.multiple_of(n * TF, TF), TF)
            hi = pl.ds(pl.multiple_of(F + n * TF, TF), TF)
            x = x1r[pl.ds(v, 2)].reshape(2 * R, D)
            g = jnp.dot(x, wgu[:, lo], preferred_element_type=F32)
            w = jnp.dot(x, wgu[:, hi], preferred_element_type=F32)
            hid[:, lo] = (g / (1.0 + jnp.exp(-g)) * w).astype(BF16)
            return 0

        def fall(n, _):
            c = pl.ds(pl.multiple_of(n * TN, TN), TN)
            y = jnp.dot(hid[...], wd[:, c], preferred_element_type=F32)
            yb[pl.ds(v, 2), :, c] = y.astype(BF16).reshape(2, R, TN)
            return 0
        lax.fori_loop(0, F // TF, rise, 0)
        lax.fori_loop(0, D // TN, fall, 0)

    x1r[0] = jnp.zeros((R, D), BF16)
    select(0)
    loads[1].wait()
    loads[2].wait()

    def step(k, _):
        acopy(0, k, 0).wait_recv()
        acopy(1, k, 0).wait_recv()
        acopy(0, k + 1, 2 * k - 1).start()

        @pl.when(k < 3)
        def _():
            acopy(1, k + 1, 2 * k).start()
        for h in range(2):
            for d in range(2):
                zcopy(d, k, h, 0).wait_recv()
                forward = functools.partial(zcopy, d, k + 1, h, 2 * k - 1 + d)
                if d == h:
                    forward().start()
                else:
                    @pl.when(k < 3)
                    def _():
                        forward().start()
        select(2 * k - 1)
        select(2 * k)

        @pl.when(k > 1)
        def _():
            xwait(x1r, x1rs, 2 * k - 2)
        xwait(x1r, x1rs, 2 * k - 1)
        ffn(2 * k - 2)
        return 0
    lax.fori_loop(1, 4, step, 0)

    acopy(0, 4, 0).wait_recv()
    zcopy(0, 4, 0, 0).wait_recv()
    zcopy(1, 4, 1, 0).wait_recv()
    select(7)
    pick(sel8[...], lambda c: ag[:, :, c].reshape(8 * T, TN), 9)
    give = functools.partial(xsend, yb, x2r, x2ss, x2rs)
    give(1)

    def tail(g, _):
        xwait(x1r, x1rs, 2 * g - 2)
        xwait(x1r, x1rs, 2 * g - 1)
        ffn(2 * g - 2)
        return 0
    lax.fori_loop(4, 6, tail, 0)
    for u in (7, 8, 5, 6, 3, 4, 1, 2):
        give(u + 1)

    def combine(u, p):
        xwait(x2r, x2rs, u + 1)
        r3 = jnp.broadcast_to(ranks[u][:, None, :], (J, SLOT, T))
        g3 = jnp.broadcast_to(gates[u][:, None, :], (J, SLOT, T))
        c0 = jnp.where(r3 == slot3, g3, 0.0).reshape(R, T).T
        c8 = (jnp.where(r3 == float(SLOT), g3, 0.0)
              * jnp.where(slot3 == float(u), 1.0, 0.0)).reshape(R, T).T
        hi0, hi8 = c0.astype(BF16), c8.astype(BF16)
        lo0, lo8 = (c0 - hi0.astype(F32)).astype(BF16), (c8 - hi8.astype(F32)).astype(BF16)

        def tile(n, _):
            c = pl.ds(pl.multiple_of(n * TN, TN), TN)
            main, extra = x2r[u + 1, :, c], x2r[9, :, c]
            total = jnp.dot(hi0, main, preferred_element_type=F32)
            total += jnp.dot(lo0, main, preferred_element_type=F32)
            total += jnp.dot(hi8, extra, preferred_element_type=F32)
            total += jnp.dot(lo8, extra, preferred_element_type=F32)
            pf[p, :, c] = total
            return 0
        lax.fori_loop(0, D // TN, tile, 0)

    def rcopy(u, h, target):
        return remote(rss.at[u, half[h]], rsr.at[u, half[h]], rsss.at[u, h], rsrs.at[u, h], target)

    def pass_on(u, p, h, source, target):
        total = pf[p, half[h], :]
        if source is not None:
            rcopy(source, h, target).wait_recv()
            total = total + rsr[source, half[h], :].astype(F32)
        rss[u, half[h], :] = total.astype(BF16)
        rcopy(u, h, target).start()

    xwait(x2r, x2rs, 9)
    combine(7, 0)
    pass_on(7, 0, 0, None, dn)
    pass_on(7, 0, 1, None, up)
    combine(5, 0)
    pass_on(5, 0, 1, None, dn)
    combine(6, 1)
    pass_on(6, 1, 0, None, up)
    pass_on(5, 0, 0, 7, dn)
    pass_on(6, 1, 1, 7, up)
    for u in (3, 1):
        combine(u, 0)
        combine(u + 1, 1)
        for h in (1, 0):
            pass_on(u, 0, h, u + 2, dn)
            pass_on(u + 1, 1, 1 - h, u + 3, up)
    combine(0, 0)
    for h in range(2):
        rcopy(1, h, dn).wait_recv()
        rcopy(2, h, dn).wait_recv()
        total = (pf[0, half[h], :] + rsr[1, half[h], :].astype(F32)
                 + rsr[2, half[h], :].astype(F32))
        out[0, half[h], :] = (arr[half[h], :].astype(F32) + total).astype(BF16)

    for c in ycopies:
        c.wait_send()
    for k in range(1, 5):
        for d in range(2):
            if k < 4 or d == 0:
                acopy(d, k, 0).wait_send()
            for h in range(2):
                if k < 4 or d == h:
                    zcopy(d, k, h, 0).wait_send()
    for u in range(9):
        xwait(x1s, x1ss, u + 1)
        xwait(yb, x2ss, u + 1)
    for u in range(1, 8):
        for h in range(2):
            rcopy(u, h, dn).wait_send()


def body(J, fresh, previous, norm_gain, routes, gate_weights, w_gate_up, w_down):
    T, D = fresh.shape
    F = w_down.shape[2]
    K = routes.shape[2]
    Z = lax.axis_size("expert") // J
    R = J * SLOT
    pad = jnp.zeros((8 - K, T), F32)
    aux = jnp.concatenate(
        [routes[0].T.astype(F32), pad - 1.0, gate_weights[0].T, pad], axis=0)
    anywhere, vmem = pl.BlockSpec(memory_space=pl.ANY), pl.BlockSpec(memory_space=pltpu.VMEM)
    dma = pltpu.SemaphoreType.DMA
    return pl.pallas_call(
        functools.partial(kernel, Z, J, K),
        out_shape=jax.ShapeDtypeStruct((1, T, D), BF16),
        in_specs=[anywhere, anywhere, vmem, vmem, anywhere, anywhere],
        out_specs=vmem,
        scratch_shapes=[
            pltpu.VMEM((D, 2 * F), BF16), pltpu.VMEM((F, D), BF16),
            pltpu.VMEM((T, D), BF16), pltpu.VMEM((T, D), BF16), pltpu.VMEM((T, D), BF16),
            pltpu.VMEM((8, T, D), BF16), pltpu.VMEM((8, 16, T), F32),
            pltpu.VMEM((10, R, D), BF16), pltpu.VMEM((10, R, D), BF16),
            pltpu.VMEM((10, R, D), BF16), pltpu.VMEM((10, R, D), BF16),
            pltpu.VMEM((8, T, D), BF16), pltpu.VMEM((8, T, D), BF16),
            pltpu.VMEM((2 * R, F), BF16), pltpu.VMEM((2, T, D), F32),
            pltpu.VMEM((R, 8 * T), BF16), pltpu.VMEM((8, J, T), F32), pltpu.VMEM((8, J, T), F32),
            dma((2,)), dma((2,)), dma((3,)), dma((2, 4, 2)), dma((2, 4, 2)), dma((2, 4)),
            dma((2, 4)), dma((10,)), dma((10,)), dma((10,)), dma((10,)), dma((8, 2)), dma((8, 2)),
        ],
        compiler_params=pltpu.CompilerParams(
            collective_id=0, has_side_effects=True, vmem_limit_bytes=62 * 2**20),
    )(previous, fresh, norm_gain, aux, w_gate_up, w_down)


def solution(mesh):
    blocks = 8
    return jax.shard_map(
        functools.partial(body, mesh.shape["expert"] // blocks),
        mesh=mesh,
        in_specs=(
            P("expert", None),
            P("section", "expert", None),
            P("section", None),
            P("section", "expert", None),
            P("section", "expert", None),
            P("section", "expert", None, None),
            P("section", "expert", None, None),
        ),
        out_specs=P("section", "expert", None),
        check_vma=False,
    )
```

```python
import functools

import jax
import jax.numpy as jnp
from jax import lax
from jax.experimental import pallas as pl
from jax.experimental.pallas import tpu as pltpu
from jax.sharding import PartitionSpec as P

EPS = 1e-06
SLOT = 16
PIECES = 4
RETURNS = (
    (7, 0), (8, 0), (3, 0), (4, 0), (1, 0), (2, 0), (7, 1), (8, 1), (5, 1), (6, 1), (3, 1), (4, 1),
    (1, 1), (2, 1), (0, 0), (0, 1),
)
MESH = pl.DeviceIdType.MESH
F32, BF16 = jnp.float32, jnp.bfloat16


def kernel(
    Z, J,
    prev, fresh, gain, routes, weights, wgu_h, wd_h, out,
    wgu, wd, fr, yr, arr, ag, auxb, x1s, x1r, x1e, x1f, yb, ye, x2r, x2e, rss, rsr, hid, pf,
    sel8, ranks, gates,
    ysem, yrem, lsem, zss, zrs, axs, axr, x1ss, x1rs, x2ss, x2rs, rsss, rsrs,
):
    T, D = arr.shape
    K = routes.shape[0]
    F = wd.shape[0]
    R = J * SLOT
    CW, TN, TF = D // 2, D // 4, min(256, F)
    sec, nsec = lax.axis_index("section"), lax.axis_size("section")
    e = lax.axis_index("expert")
    z, j = lax.div(e, J), lax.rem(e, J)
    up = lax.rem(z + 1, Z) * J + j
    dn = lax.rem(z + Z - 1, Z) * J + j
    ynext, yprev = lax.rem(sec + 1, nsec), lax.rem(sec + nsec - 1, nsec)
    toward = (up, dn)
    piece = [pl.ds(p * (T // PIECES), T // PIECES) for p in range(PIECES)]
    order = [q for q in (4, 2, 6, 5, 3, 7, 1) if q < J]

    def remote(src, dst, ssem, rsem, expert):
        return pltpu.make_async_remote_copy(
            src_ref=src, dst_ref=dst, send_sem=ssem, recv_sem=rsem,
            device_id={"expert": expert}, device_id_type=MESH)

    def columns(n, width):
        return pl.ds(pl.multiple_of(n * width, width), width)

    barrier = pltpu.get_barrier_semaphore()
    for t in (ynext, yprev):
        pl.semaphore_signal(barrier, inc=1, device_id={"section": t}, device_id_type=MESH)
    for t in (up, dn):
        pl.semaphore_signal(barrier, inc=1, device_id={"expert": t}, device_id_type=MESH)
    for q in order:
        pl.semaphore_signal(
            barrier, inc=1, device_id={"expert": z * J + lax.rem(j + q, J)}, device_id_type=MESH)

    loads = (
        pltpu.make_async_copy(fresh, fr, lsem.at[0]),
        pltpu.make_async_copy(wgu_h.at[0, 0], wgu, lsem.at[1]),
        pltpu.make_async_copy(wd_h.at[0, 0], wd, lsem.at[2]),
    )
    loads[0].start()
    auxb[0] = jnp.full((16, T), -1.0, F32)
    auxb[0, 0:K, :] = routes[...].astype(F32)
    auxb[0, 8:8 + K, :] = weights[...]
    pl.semaphore_wait(barrier, 4 + len(order))

    ycopies = [
        pltpu.make_async_remote_copy(
            src_ref=prev.at[0, piece[p]], dst_ref=yr.at[piece[p]], send_sem=ysem.at[p],
            recv_sem=yrem.at[p], device_id={"section": ynext}, device_id_type=MESH)
        for p in range(PIECES)
    ]
    for c in ycopies:
        c.start()

    def zcopy(d, k, p, src):
        dst = 2 * k - 1 if d == 0 else jnp.minimum(2 * k, 7)
        return remote(ag.at[src, piece[p]], ag.at[dst, piece[p]], zss.at[d, k - 1, p],
                      zrs.at[d, k - 1, p], toward[d])

    def acopy(d, k, src):
        dst = 2 * k - 1 if d == 0 else jnp.minimum(2 * k, 7)
        return remote(auxb.at[src], auxb.at[dst], axs.at[d, k - 1], axr.at[d, k - 1], toward[d])

    def last_hop(d, p):
        return (p < PIECES // 2) == (d == 0)

    acopy(0, 1, 0).start()
    acopy(1, 1, 0).start()
    loads[1].start()
    loads[2].start()
    loads[0].wait()
    for p in range(PIECES):
        ycopies[p].wait_recv()
        x = jnp.where(sec == 0, fr[piece[p], :].astype(F32), yr[piece[p], :].astype(F32))
        arr[piece[p], :] = x.astype(BF16)
        scale = lax.rsqrt(jnp.mean(x * x, axis=-1, keepdims=True) + EPS)
        ag[0, piece[p], :] = (x * scale * gain[...]).astype(BF16)
        zcopy(0, 1, p, 0).start()
        zcopy(1, 1, p, 0).start()

    slot3 = lax.broadcasted_iota(jnp.int32, (J, SLOT, T), 1).astype(F32)
    slot3h = jnp.where(slot3 >= 8.0, slot3 - 8.0, slot3)
    first = (z * J).astype(F32)

    def own_rows(q):
        return pl.ds(pl.multiple_of(q * SLOT, SLOT), SLOT)

    def xwait(buf, cols, sem):
        part = buf.at[pl.ds(0, R - SLOT), cols]
        pltpu.make_async_copy(part, part, sem).wait()

    def exchange(src, dst, cols, ssem, rsem):
        dst[own_rows(j), cols] = src[own_rows(j), cols]
        for q in order:
            pj = lax.rem(j + q, J)
            remote(src.at[own_rows(pj), cols], dst.at[own_rows(j), cols], ssem, rsem,
                   z * J + pj).start()

    full, packed = pl.ds(0, D), pl.ds(0, CW)

    def select(u):
        a = auxb[u]
        expert = lax.broadcasted_iota(jnp.int32, (J, T), 0).astype(F32) + first
        mask, gate = jnp.zeros((J, T), F32), jnp.zeros((J, T), F32)
        for k in range(K):
            hit = a[k:k + 1, :] == expert
            mask = mask + jnp.where(hit, 1.0, 0.0)
            gate = gate + jnp.where(hit, a[8 + k:9 + k, :], 0.0)
        before = (lax.broadcasted_iota(jnp.int32, (T, T), 0)
                  < lax.broadcasted_iota(jnp.int32, (T, T), 1))
        tri = jnp.where(before, 1.0, 0.0).astype(BF16)
        rank = jnp.dot(mask.astype(BF16), tri, preferred_element_type=F32)
        rank = jnp.where(mask > 0.5, rank, -1.0)
        ranks[u] = rank
        gates[u] = gate
        r3 = jnp.broadcast_to(rank[:, None, :], (J, SLOT, T))
        uf = jnp.asarray(u, jnp.int32).astype(F32)
        sel = jnp.where(r3 == slot3, 1.0, 0.0).reshape(R, T).astype(BF16)
        extra = jnp.where(r3 == float(SLOT), 1.0, 0.0) * jnp.where(slot3h == uf, 1.0, 0.0)
        sel8[:, columns(u, T)] = extra.reshape(R, T).astype(BF16)

        def tile(n, _):
            c = columns(n, TN)
            x1s[u, :, c] = jnp.dot(sel, ag[u, :, c], preferred_element_type=F32).astype(BF16)
            return 0
        lax.fori_loop(0, D // TN, tile, 0)
        exchange(x1s.at[u], x1r.at[u + 1], full, x1ss.at[u], x1rs.at[u])

    low = lax.rem(lax.broadcasted_iota(jnp.int32, (R, TN), 0), SLOT) < 8

    def mover(shift, upper):
        r = lax.broadcasted_iota(jnp.int32, (R, R), 0)
        c = lax.broadcasted_iota(jnp.int32, (R, R), 1)
        wanted = (lax.rem(r, SLOT) >= 8) if upper else (lax.rem(r, SLOT) < 8)
        return jnp.where(wanted, jnp.where(c == r + shift, 1.0, 0.0), 0.0).astype(BF16)

    def select_extra():
        def tile(h, _):
            a = jnp.dot(sel8[...], ag[:, :, columns(2 * h, TN)].reshape(8 * T, TN),
                        preferred_element_type=F32)
            b = jnp.dot(sel8[...], ag[:, :, columns(2 * h + 1, TN)].reshape(8 * T, TN),
                        preferred_element_type=F32)
            x1e[:, columns(h, TN)] = jnp.where(low, a, b).astype(BF16)
            return 0
        lax.fori_loop(0, 2, tile, 0)
        exchange(x1e, x1f, packed, x1ss.at[8], x1rs.at[8])

    def spread_extra():
        down = mover(8, False)

        def tile(h, _):
            a = x1f[:, columns(h, TN)]
            x1r[9, :, columns(2 * h, TN)] = a
            x1r[9, :, columns(2 * h + 1, TN)] = jnp.dot(
                down, a, preferred_element_type=F32).astype(BF16)
            return 0
        lax.fori_loop(0, 2, tile, 0)

    def pack_extra():
        raised = mover(-8, True)

        def tile(h, _):
            a = yb[9, :, columns(2 * h, TN)].astype(F32)
            b = jnp.dot(raised, yb[9, :, columns(2 * h + 1, TN)], preferred_element_type=F32)
            ye[:, columns(h, TN)] = jnp.where(low, a, b).astype(BF16)
            return 0
        lax.fori_loop(0, 2, tile, 0)

    def ffn(v):
        def rise(n, _):
            lo = columns(n, TF)
            hi = pl.ds(pl.multiple_of(F + n * TF, TF), TF)
            x = x1r[pl.ds(v, 2)].reshape(2 * R, D)
            g = jnp.dot(x, wgu[:, lo], preferred_element_type=F32)
            w = jnp.dot(x, wgu[:, hi], preferred_element_type=F32)
            hid[:, lo] = (g / (1.0 + jnp.exp(-g)) * w).astype(BF16)
            return 0

        def fall(n, _):
            c = columns(n, TN)
            y = jnp.dot(hid[...], wd[:, c], preferred_element_type=F32)
            yb[pl.ds(v, 2), :, c] = y.astype(BF16).reshape(2, R, TN)
            return 0
        lax.fori_loop(0, F // TF, rise, 0)
        lax.fori_loop(0, D // TN, fall, 0)

    x1r[0] = jnp.zeros((R, D), BF16)
    select(0)
    loads[1].wait()
    loads[2].wait()

    def step(k, _):
        acopy(0, k, 0).wait_recv()
        acopy(1, k, 0).wait_recv()
        acopy(0, k + 1, 2 * k - 1).start()

        @pl.when(k < 3)
        def _():
            acopy(1, k + 1, 2 * k).start()
        for p in range(PIECES):
            for d in range(2):
                zcopy(d, k, p, 0).wait_recv()
                forward = functools.partial(zcopy, d, k + 1, p, 2 * k - 1 + d)
                if last_hop(d, p):
                    forward().start()
                else:
                    @pl.when(k < 3)
                    def _():
                        forward().start()
        select(2 * k - 1)
        select(2 * k)

        @pl.when(k > 1)
        def _():
            xwait(x1r.at[2 * k - 2], full, x1rs.at[2 * k - 3])
        xwait(x1r.at[2 * k - 1], full, x1rs.at[2 * k - 2])
        ffn(2 * k - 2)
        return 0
    lax.fori_loop(1, 4, step, 0)

    acopy(0, 4, 0).wait_recv()
    for p in range(PIECES):
        zcopy(0 if last_hop(0, p) else 1, 4, p, 0).wait_recv()
    select(7)
    select_extra()

    def give(u, h):
        if u < 8:
            exchange(yb.at[u + 1], x2r.at[u], columns(h, CW), x2ss.at[u, h], x2rs.at[u, h])
        else:
            exchange(ye, x2e, columns(h, TN), x2ss.at[u, h], x2rs.at[u, h])

    def tail(g, _):
        xwait(x1r.at[2 * g - 2], full, x1rs.at[2 * g - 3])

        @pl.when(g == 4)
        def _():
            xwait(x1r.at[7], full, x1rs.at[6])

        @pl.when(g == 5)
        def _():
            xwait(x1f, packed, x1rs.at[8])
            spread_extra()
        ffn(2 * g - 2)

        @pl.when(g == 4)
        def _():
            give(5, 0)
            give(6, 0)
        return 0
    lax.fori_loop(4, 6, tail, 0)
    pack_extra()
    for u, h in RETURNS:
        give(u, h)

    def combine(u, p, h):
        xwait(x2r.at[u], columns(h, CW), x2rs.at[u, h])
        r3 = jnp.broadcast_to(ranks[u][:, None, :], (J, SLOT, T))
        g3 = jnp.broadcast_to(gates[u][:, None, :], (J, SLOT, T))
        over = jnp.where(r3 == float(SLOT), g3, 0.0)
        parts = [jnp.where(r3 == slot3, g3, 0.0)]
        parts += [jnp.where(slot3 == float(u + 8 * i), over, 0.0) for i in range(2)]
        parts = [c.reshape(R, T).T for c in parts]
        high = [c.astype(BF16) for c in parts]
        rest = [(c - b.astype(F32)).astype(BF16) for c, b in zip(parts, high)]
        extra = x2e[:, columns(h, TN)]
        for i in range(2):
            main = x2r[u, :, columns(2 * h + i, TN)]
            total = jnp.dot(high[0], main, preferred_element_type=F32)
            total += jnp.dot(rest[0], main, preferred_element_type=F32)
            total += jnp.dot(high[1 + i], extra, preferred_element_type=F32)
            total += jnp.dot(rest[1 + i], extra, preferred_element_type=F32)
            pf[p, :, pl.ds(i * TN, TN)] = total

    def rcopy(u, h, target):
        return remote(rss.at[u, h], rsr.at[u, h], rsss.at[u, h], rsrs.at[u, h], target)

    def take(source, p, h, target):
        rcopy(source, h, target).wait_recv()
        pf[p] = pf[p] + rsr[source, h].astype(F32)

    def send_on(u, p, h, target):
        rss[u, h] = pf[p].astype(BF16)
        rcopy(u, h, target).start()

    def reduce_half(h, _):
        xwait(x2e, columns(h, TN), x2rs.at[8, h])
        combine(7, 0, h)
        send_on(7, 0, h, jnp.where(h == 0, dn, up))
        combine(5, 0, h)
        combine(6, 1, h)

        @pl.when(h == 0)
        def _():
            send_on(6, 1, h, up)
            take(7, 0, h, dn)
            send_on(5, 0, h, dn)

        @pl.when(h == 1)
        def _():
            send_on(5, 0, h, dn)
            take(7, 1, h, up)
            send_on(6, 1, h, up)
        for u in (3, 1):
            combine(u, 0, h)
            combine(u + 1, 1, h)
            take(u + 2, 0, h, dn)
            send_on(u, 0, h, dn)
            take(u + 3, 1, h, up)
            send_on(u + 1, 1, h, up)
        return 0
    lax.fori_loop(0, 2, reduce_half, 0)

    def finish(h, _):
        c = columns(h, CW)
        combine(0, 0, h)
        take(1, 0, h, dn)
        take(2, 0, h, up)
        out[0, :, c] = (arr[:, c].astype(F32) + pf[0]).astype(BF16)
        return 0
    lax.fori_loop(0, 2, finish, 0)

    for c in ycopies:
        c.wait_send()
    for k in range(1, 5):
        for d in range(2):
            if k < 4 or d == 0:
                acopy(d, k, 0).wait_send()
            for p in range(PIECES):
                if k < 4 or last_hop(d, p):
                    zcopy(d, k, p, 0).wait_send()
    for u in range(8):
        xwait(x1s.at[u], full, x1ss.at[u])
    xwait(x1e, packed, x1ss.at[8])
    for h in range(2):
        for u in range(8):
            xwait(x2r.at[u], columns(h, CW), x2ss.at[u, h])
        xwait(ye, columns(h, TN), x2ss.at[8, h])
        for u in range(1, 8):
            rcopy(u, h, dn).wait_send()


def body(J, fresh, previous, norm_gain, routes, gate_weights, w_gate_up, w_down):
    T, D = fresh.shape
    F = w_down.shape[2]
    Z = lax.axis_size("expert") // J
    R = J * SLOT
    anywhere, vmem = pl.BlockSpec(memory_space=pl.ANY), pl.BlockSpec(memory_space=pltpu.VMEM)
    dma = pltpu.SemaphoreType.DMA
    return pl.pallas_call(
        functools.partial(kernel, Z, J),
        out_shape=jax.ShapeDtypeStruct((1, T, D), BF16),
        in_specs=[anywhere, anywhere, vmem, vmem, vmem, anywhere, anywhere],
        out_specs=vmem,
        scratch_shapes=[
            pltpu.VMEM((D, 2 * F), BF16), pltpu.VMEM((F, D), BF16),
            pltpu.VMEM((T, D), BF16), pltpu.VMEM((T, D), BF16), pltpu.VMEM((T, D), BF16),
            pltpu.VMEM((8, T, D), BF16), pltpu.VMEM((8, 16, T), F32),
            pltpu.VMEM((8, R, D), BF16), pltpu.VMEM((10, R, D), BF16),
            pltpu.VMEM((R, D // 2), BF16), pltpu.VMEM((R, D // 2), BF16),
            pltpu.VMEM((10, R, D), BF16), pltpu.VMEM((R, D // 2), BF16),
            pltpu.VMEM((8, R, D), BF16), pltpu.VMEM((R, D // 2), BF16),
            pltpu.VMEM((8, 2, T, D // 2), BF16), pltpu.VMEM((8, 2, T, D // 2), BF16),
            pltpu.VMEM((2 * R, F), BF16), pltpu.VMEM((2, T, D // 2), F32),
            pltpu.VMEM((R, 8 * T), BF16), pltpu.VMEM((8, J, T), F32), pltpu.VMEM((8, J, T), F32),
            dma((PIECES,)), dma((PIECES,)), dma((3,)), dma((2, 4, PIECES)), dma((2, 4, PIECES)),
            dma((2, 4)), dma((2, 4)), dma((9,)), dma((9,)), dma((9, 2)), dma((9, 2)),
            dma((8, 2)), dma((8, 2)),
        ],
        compiler_params=pltpu.CompilerParams(
            collective_id=0, has_side_effects=True, vmem_limit_bytes=62 * 2**20),
    )(previous, fresh, norm_gain, routes[0].T, gate_weights[0].T, w_gate_up, w_down)


def solution(mesh):
    blocks = 8
    return jax.shard_map(
        functools.partial(body, mesh.shape["expert"] // blocks),
        mesh=mesh,
        in_specs=(
            P("expert", None),
            P("section", "expert", None),
            P("section", None),
            P("section", "expert", None),
            P("section", "expert", None),
            P("section", "expert", None, None),
            P("section", "expert", None, None),
        ),
        out_specs=P("section", "expert", None),
        check_vma=False,
    )
```
